128 devices in a mesh: hst: 4 (over z), dev: 32 (over y, x, core).
Axes of the slice: x: 4, y: 4, z: 4, core: 2. Of those that a mesh axis runs over, the one named last changes fastest.
Arguments:
- features: bfloat16 [262144, 768], P(('hst', 'dev')), may hold values from -6 to 6
- cache_blocks: bfloat16 [4, 8192, 768], P('hst', 'dev'), may hold values from -6 to 6
- plan: int32 [4, 64], P('hst', 'dev'), may hold values from 0 to 63, as said below
- miss_ids: int32 [128, 4, 32, 16], P(('hst', 'dev')), may hold values from 0 to 2303, as said below
- miss_counts: int32 [128, 4, 32], P(('hst', 'dev')), may hold values from 4 to 16, as said below
- self_ids: int32 [106496], P(('hst', 'dev')), may hold values from 0 to 2047, as said below
- nbr_ids: int32 [106496, 15], P(('hst', 'dev')), may hold values from 0 to 2047, as said below
- hop_counts: int32 [106496], P(('hst', 'dev')), may hold values from 1 to 15, as said below
- seed_counts: int32 [4096], P(('hst', 'dev')), may hold values from 1 to 25, as said below
- w_self1: bfloat16 [768, 1024], replicated, may hold values from -0.21875 to 0.21875
- w_nbr1: bfloat16 [768, 1024], replicated, may hold values from -0.21875 to 0.21875
- w_self2: bfloat16 [1024, 1024], replicated, may hold values from -0.1875 to 0.1875
- w_nbr2: bfloat16 [1024, 1024], replicated, may hold values from -0.1875 to 0.1875
- cotangent: bfloat16 [4096, 1024], P(('hst', 'dev')), may hold values from -1.25 to 1.25
Outputs:
- embedding: bfloat16 [4096, 1024], P(('hst', 'dev'))
- new_cache: bfloat16 [4, 8192, 768], P('hst', 'dev')
- grad_self1: float32 [768, 1024], P(None, ('hst', 'dev'))
- grad_nbr1: float32 [768, 1024], P(None, ('hst', 'dev'))
- grad_self2: float32 [1024, 1024], P(None, ('hst', 'dev'))
- grad_nbr2: float32 [1024, 1024], P(None, ('hst', 'dev'))
The draws below stay inside these ranges and needn't reach their ends.
Inputs may be any that keep to these rules, and one draw needn't show every extreme that they name: Within each cache domain h, plan[h] is a permutation of the 64 block numbers. `miss_ids`: row numbers into the peer's served table; slots at or past the count are unused. `miss_counts`: in every draw some peer is asked for 16 rows by every device. `self_ids`: each names a used fetched slot p * 16 + c of the same device, c below that device's count for peer p. `nbr_ids`: each names a used fetched slot p * 16 + c of the same device, c below that device's count for peer p. `hop_counts`: the first node of every device has 15. `seed_counts`: the first seed of every device has 25.
All inputs are finite; a program needn't handle non-finite values.
Results may differ from the reference program's by a relative error of at most 0.0052.
Values may be sent and summed in bfloat16 or wider, within the bound.
No kernel may reach another device: no remote copies, remote signals or barrier semaphores. Data moves between devices by JAX's collectives and lax.ppermute only.
A program may use at most 128 MiB of HBM per device.

```python
import jax
import jax.numpy as jnp
from jax import lax

F = 768
H = 1024
FAN1 = 25
FAN2 = 15
SEED_DEV = 32
ROWS_DEV = 2048
CSLOT = 2
BLOCK = 128
CAP = 16
T1 = 832
NODES = 262144
SEEDS = 4096
N_HST = 4
N_DEV = 32


def fill_counts(key):
    device_count = N_HST * N_DEV
    lowest = max(CAP // 4, 1)
    counts = jax.random.randint(jax.random.fold_in(key, 11), (device_count, device_count), lowest, CAP + 1, dtype=jnp.int32)
    hot_peer = jax.random.randint(jax.random.fold_in(key, 12), (), 0, device_count, dtype=jnp.int32)
    counts = counts.at[:, hot_peer].set(CAP)
    return counts


def frontier_refs(key):
    device_count = N_HST * N_DEV
    counts = fill_counts(key)
    peer_pick = jax.random.randint(jax.random.fold_in(key, 31), (device_count, T1, FAN2 + 1), 0, device_count, dtype=jnp.int32)
    raw_bits = jax.random.randint(jax.random.fold_in(key, 32), (device_count, T1, FAN2 + 1), 0, 1 << 20, dtype=jnp.int32)
    device_index = jnp.arange(device_count, dtype=jnp.int32)[:, None, None]
    limit = counts[device_index, peer_pick]
    return (peer_pick * CAP + raw_bits % limit).astype(jnp.int32)


def draw_miss_counts(key, part):
    return fill_counts(key).reshape(N_HST * N_DEV, N_HST, N_DEV)


def draw_miss_ids(key, part):
    shape = (N_HST * N_DEV, N_HST, N_DEV, CAP)
    coin = jax.random.randint(jax.random.fold_in(key, 13), shape, 0, 2, dtype=jnp.int32)
    cached = ROWS_DEV + jax.random.randint(jax.random.fold_in(key, 14), shape, 0, CSLOT * BLOCK, dtype=jnp.int32)
    stored = jax.random.randint(jax.random.fold_in(key, 15), shape, 0, ROWS_DEV, dtype=jnp.int32)
    return jnp.where(coin == 1, cached, stored).astype(jnp.int32)


def draw_self_ids(key, part):
    return frontier_refs(key)[:, :, 0].reshape(N_HST * N_DEV * T1)


def draw_nbr_ids(key, part):
    return frontier_refs(key)[:, :, 1:].reshape(N_HST * N_DEV * T1, FAN2)


def draw_hop_counts(key, part):
    counts = jax.random.randint(jax.random.fold_in(key, 41), (N_HST * N_DEV, T1), 1, FAN2 + 1, dtype=jnp.int32)
    return counts.at[:, 0].set(FAN2).reshape(N_HST * N_DEV * T1)


def draw_seed_counts(key, part):
    counts = jax.random.randint(jax.random.fold_in(key, 42), (N_HST * N_DEV, SEED_DEV), 1, FAN1 + 1, dtype=jnp.int32)
    return counts.at[:, 0].set(FAN1).reshape(N_HST * N_DEV * SEED_DEV)


def draw_plan(key, part):
    host_keys = jax.random.split(jax.random.fold_in(key, 21), N_HST)
    orders = jax.vmap(lambda host_key: jax.random.permutation(host_key, N_DEV * CSLOT))(host_keys)
    return orders.astype(jnp.int32)


def with_spikes(values, own_key, source, target, blocks, factor):
    owner, partner = [(jnp.arange(values.shape[axis_at]) // (values.shape[axis_at] // blocks)).reshape([-1 if axis == axis_at else 1 for axis in range(values.ndim)]) for axis_at in (source, target)]
    chosen = jax.random.permutation(own_key, blocks)[partner]
    strong = (owner == chosen) | (owner == (partner + blocks // 2) % blocks)
    return jnp.where(strong, factor * values, values)


def block_scale(own_key, shape, pieces, least, largest):
    def one(position, parts):
        heights = jax.random.uniform(jax.random.fold_in(jax.random.fold_in(own_key, 6), position), (parts,), jnp.float32, least / len(pieces), largest / len(pieces))
        return jnp.repeat(jnp.exp(heights), shape[position] // parts).reshape((-1,) + (1,) * (len(shape) - position - 1))

    factor_of = one(*pieces[0])
    for cut in pieces[1:]:
        factor_of = factor_of * one(*cut)
    return factor_of


def normal_values(stream_key, extent, width, bound, pieces=(), held_as=jnp.bfloat16):
    values = jax.random.normal(stream_key, extent, jnp.float32) * width
    if len(pieces) > 0:
        values = block_scale(stream_key, extent, pieces, -0.22, 0.18) * values
    return jnp.clip(values, min=-bound, max=bound).astype(held_as)


def gaussian_with(own_key, dims, scale, most, pieces, heavy, held_as=jnp.bfloat16):
    entries = scale * jax.random.normal(own_key, dims, jnp.float32)
    if pieces:
        entries = entries * block_scale(own_key, dims, pieces, -0.22, 0.18)
    return jnp.clip(with_spikes(entries, jax.random.fold_in(own_key, 3), *heavy), -most, most).astype(held_as)


def setup_inputs(seed: int = 0) -> dict:
    splits = jax.random.split(jax.random.key(seed), 15)
    return {
        "features": normal_values(splits[0], (NODES, F), 1.0, 6.0, ((0, 128),)),
        "cache_blocks": normal_values(splits[1], (N_HST, N_DEV * CSLOT * BLOCK, F), 1.0, 6.0, ((0, 4), (1, 32))),
        "plan": draw_plan(jax.random.fold_in(splits[14], 71), 0),
        "miss_ids": draw_miss_ids(jax.random.fold_in(splits[14], 71), 0),
        "miss_counts": draw_miss_counts(jax.random.fold_in(splits[14], 71), 0),
        "self_ids": draw_self_ids(jax.random.fold_in(splits[14], 71), 0),
        "nbr_ids": draw_nbr_ids(jax.random.fold_in(splits[14], 71), 0),
        "hop_counts": draw_hop_counts(jax.random.fold_in(splits[14], 71), 0),
        "seed_counts": draw_seed_counts(jax.random.fold_in(splits[14], 71), 0),
        "w_self1": normal_values(splits[9], (F, H), F ** -0.5, 0.21875),
        "w_nbr1": normal_values(splits[10], (F, H), F ** -0.5, 0.21875),
        "w_self2": normal_values(splits[11], (H, H), H ** -0.5, 0.1875),
        "w_nbr2": normal_values(splits[12], (H, H), H ** -0.5, 0.1875),
        "cotangent": gaussian_with(splits[13], (SEEDS, H), 0.05, 1.25, ((0, 128),), (0, 1, 128, 5.5)),
    }


def local_step(frontier, self_rows, nbr_rows, count_one, count_two, w_self1, w_nbr1, w_self2, w_nbr2, cot_rows):
    own_rows = frontier[self_rows]
    mask_one = (jnp.arange(FAN2, dtype=jnp.int32)[None, :] < count_one[:, None])
    summed_one = jnp.zeros((own_rows.shape[0], F), jnp.float32)
    for k in range(FAN2):
        picked = frontier[nbr_rows[:, k]].astype(jnp.float32)
        summed_one = summed_one + jnp.where(mask_one[:, k][:, None], picked, jnp.zeros_like(picked))
    mean_one = (summed_one / count_one[:, None].astype(jnp.float32)).astype(jnp.bfloat16)
    hidden_pre = jnp.dot(own_rows, w_self1, preferred_element_type=jnp.float32) + jnp.dot(mean_one, w_nbr1, preferred_element_type=jnp.float32)
    hidden_one = jax.nn.silu(hidden_pre).astype(jnp.bfloat16)
    seed_rows = hidden_one[:SEED_DEV]
    hop_rows = hidden_one[SEED_DEV:].reshape(SEED_DEV, FAN1, H)
    mask_two = (jnp.arange(FAN1, dtype=jnp.int32)[None, :] < count_two[:, None]).astype(jnp.float32)
    summed_two = jnp.einsum("skh,sk->sh", hop_rows.astype(jnp.float32), mask_two)
    mean_two = (summed_two / count_two[:, None].astype(jnp.float32)).astype(jnp.bfloat16)
    embedding = (jnp.dot(seed_rows, w_self2, preferred_element_type=jnp.float32) + jnp.dot(mean_two, w_nbr2, preferred_element_type=jnp.float32)).astype(jnp.bfloat16)
    grad_self2 = jnp.dot(seed_rows.T, cot_rows, preferred_element_type=jnp.float32)
    grad_nbr2 = jnp.dot(mean_two.T, cot_rows, preferred_element_type=jnp.float32)
    back_self = jnp.dot(cot_rows, w_self2.T, preferred_element_type=jnp.float32)
    back_mean = jnp.dot(cot_rows, w_nbr2.T, preferred_element_type=jnp.float32) / count_two[:, None].astype(jnp.float32)
    back_hop = back_mean[:, None, :] * mask_two[:, :, None]
    back_hidden = jnp.concatenate([back_self, back_hop.reshape(SEED_DEV * FAN1, H)], 0)
    gate_value = jax.nn.sigmoid(hidden_pre)
    back_pre = (back_hidden * gate_value * (1.0 + hidden_pre * (1.0 - gate_value))).astype(jnp.bfloat16)
    grad_self1 = jnp.dot(own_rows.T, back_pre, preferred_element_type=jnp.float32)
    grad_nbr1 = jnp.dot(mean_one.T, back_pre, preferred_element_type=jnp.float32)
    return embedding, (grad_self1, grad_nbr1, grad_self2, grad_nbr2)


def reference(features, cache_blocks, plan, miss_ids, miss_counts, self_ids, nbr_ids, hop_counts, seed_counts, w_self1, w_nbr1, w_self2, w_nbr2, cotangent):
    device_count = N_HST * N_DEV
    cache_rows = CSLOT * BLOCK
    blocks = cache_blocks.reshape(N_HST, N_DEV * CSLOT, BLOCK, F)
    moved_blocks = jax.vmap(lambda group, order: group[order])(blocks, plan)
    new_cache = moved_blocks.reshape(N_HST, N_DEV * cache_rows, F)
    full_table = jnp.concatenate([features, new_cache.reshape(device_count * cache_rows, F)], 0)
    peer_index = jnp.arange(device_count, dtype=jnp.int32)[:, None]
    slot_index = jnp.arange(CAP, dtype=jnp.int32)[None, :]
    home_rows = ROWS_DEV * device_count

    def one_device(totals, inputs):
        asked, counted, self_rows, nbr_rows, count_one, count_two, cot_rows = inputs
        global_row = jnp.where(asked < ROWS_DEV, peer_index * ROWS_DEV + asked, home_rows + peer_index * cache_rows + asked - ROWS_DEV).astype(jnp.int32)
        row_data = full_table[global_row]
        is_valid = slot_index < counted[:, None]
        row_data = jnp.where(is_valid[:, :, None], row_data, jnp.zeros_like(row_data))
        frontier = row_data.reshape(device_count * CAP, F)
        embedding, grads = local_step(frontier, self_rows, nbr_rows, count_one, count_two, w_self1, w_nbr1, w_self2, w_nbr2, cot_rows)
        totals = tuple(total + grad for total, grad in zip(totals, grads))
        return totals, embedding

    start_totals = (jnp.zeros((F, H), jnp.float32), jnp.zeros((F, H), jnp.float32), jnp.zeros((H, H), jnp.float32), jnp.zeros((H, H), jnp.float32))
    inputs = (
        miss_ids.reshape(device_count, device_count, CAP),
        miss_counts.reshape(device_count, device_count),
        self_ids.reshape(device_count, T1),
        nbr_ids.reshape(device_count, T1, FAN2),
        hop_counts.reshape(device_count, T1),
        seed_counts.reshape(device_count, SEED_DEV),
        cotangent.reshape(device_count, SEED_DEV, H),
    )
    totals, embedded = lax.scan(one_device, start_totals, inputs)
    embedding = embedded.reshape(device_count * SEED_DEV, H)
    return (embedding, new_cache, totals[0], totals[1], totals[2], totals[3])
```

```python
import jax
import jax.numpy as jnp
from jax import lax
from jax.sharding import PartitionSpec as P

FAN1 = 25
FAN2 = 15
CSLOT = 2
BLOCK = 128
ALL = ("hst", "dev")
BF = jnp.bfloat16
F32 = jnp.float32


def parity_groups(hosts, devs):
    return [
        [h * devs + 2 * i + c for h in range(hosts) for i in range(devs // 2)] for c in range(2)
    ]


def plane_groups(hosts, devs):
    return [
        [h * devs + 2 * i + c for i in range(devs // 2)] for h in range(hosts) for c in range(2)
    ]


def exchange(x, axes, groups=None):
    return lax.all_to_all(
        x, axes, split_axis=0, concat_axis=0, tiled=True, axis_index_groups=groups
    )


def swap_pair(x, devs):
    return lax.ppermute(x, "dev", [(i, i ^ 1) for i in range(devs)])


def gather_octet(x, hosts, devs):
    pair = jnp.concatenate([x, swap_pair(x, devs)], 0)
    parts = [pair]
    for k in range(1, hosts):
        parts.append(lax.ppermute(pair, "hst", [(i, (i + k) % hosts) for i in range(hosts)]))
    return jnp.concatenate(parts, 0)


def local(
    features, cache_blocks, plan, miss_ids, miss_counts, self_ids, nbr_ids, hop_counts,
    seed_counts, w_self1, w_nbr1, w_self2, w_nbr2, cotangent,
):
    hosts = lax.axis_size("hst")
    devs = lax.axis_size("dev")
    count = hosts * devs
    rows_dev, width = features.shape
    hidden = w_self2.shape[0]
    cap = miss_ids.shape[3]
    nodes = self_ids.shape[0]
    seeds = seed_counts.shape[0]
    h = lax.axis_index("hst")
    core = lax.axis_index("dev") % 2
    half = width // 2
    groups = devs // 2
    sub = BLOCK // groups

    note = jnp.concatenate(
        [miss_ids.reshape(count, cap), jnp.broadcast_to(plan, (count, CSLOT))], 1
    )
    note = exchange(note[:, None, :], ALL)[:, 0, :]
    asked = note[:, :cap].reshape(count * cap)
    order = lax.dynamic_slice_in_dim(note[:, cap:], h * devs, devs, 0).reshape(devs * CSLOT)

    pieces = cache_blocks.reshape(CSLOT, groups, sub, 2, half).transpose(3, 1, 0, 2, 4)
    pieces = exchange(pieces.reshape(devs, CSLOT * sub, half), "dev")
    pieces = pieces.reshape(devs * CSLOT, sub, half)[order]
    pieces = exchange(pieces.reshape(devs, CSLOT * sub, half), "dev")
    moved = (
        pieces.reshape(2, groups, CSLOT, sub, half)
        .transpose(2, 1, 3, 0, 4)
        .reshape(CSLOT * BLOCK, width)
    )

    stored = features[jnp.minimum(asked, rows_dev - 1)]
    pick = ((asked - rows_dev)[:, None] == jnp.arange(CSLOT * BLOCK, dtype=jnp.int32)).astype(BF)
    cached = jnp.dot(pick, moved, preferred_element_type=F32).astype(BF)
    served = jnp.where((asked < rows_dev)[:, None], stored, cached)
    fetched = exchange(served.reshape(count, cap, width), ALL).reshape(count * cap, width)

    slot = jnp.arange(count * cap, dtype=jnp.int32)
    used = (jnp.arange(cap, dtype=jnp.int32) < miss_counts.reshape(count, 1)).reshape(-1)
    used = used.astype(BF)
    pick_self = (self_ids[:, None] == slot).astype(BF) * used
    named = jnp.where(jnp.arange(FAN2, dtype=jnp.int32) < hop_counts[:, None], nbr_ids, -1)
    pick_nbr = jnp.zeros((nodes, count * cap), BF)
    for k in range(FAN2):
        pick_nbr = pick_nbr + (named[:, k][:, None] == slot).astype(BF)
    pick_nbr = pick_nbr * used

    own = jnp.dot(pick_self, fetched, preferred_element_type=F32).astype(BF)
    total = jnp.dot(pick_nbr, fetched, preferred_element_type=F32)
    mean_one = (total / hop_counts[:, None].astype(F32)).astype(BF)
    pre = jnp.dot(own, w_self1, preferred_element_type=F32) + jnp.dot(
        mean_one, w_nbr1, preferred_element_type=F32
    )
    gate = jax.nn.sigmoid(pre)
    hidden_one = (pre * gate).astype(BF)
    seed_rows = hidden_one[:seeds]

    position = jnp.arange(nodes, dtype=jnp.int32) - seeds
    owner = jnp.where(position >= 0, position // FAN1, -1)
    live = (owner == jnp.arange(seeds, dtype=jnp.int32)[:, None]) & (
        position % FAN1 < seed_counts[:, None]
    )
    live = live.astype(BF)
    seed_float = seed_counts[:, None].astype(F32)
    total_two = jnp.dot(live, hidden_one, preferred_element_type=F32)
    mean_two = (total_two / seed_float).astype(BF)
    embedding = (
        jnp.dot(seed_rows, w_self2, preferred_element_type=F32)
        + jnp.dot(mean_two, w_nbr2, preferred_element_type=F32)
    ).astype(BF)

    cot_rows = gather_octet(cotangent, hosts, devs)
    cot_rows = lax.dynamic_slice_in_dim(cot_rows, h * (hidden // hosts), hidden // hosts, 1)
    both = gather_octet(jnp.concatenate([seed_rows, mean_two], 1), hosts, devs)
    part_two = lax.dot_general(
        cot_rows, both, (((0,), (0,)), ((), ())), preferred_element_type=F32
    )
    cols = hidden // count
    part_two = part_two.reshape(groups, 2, cols, 2 * hidden)
    part_two = lax.dynamic_index_in_dim(part_two, core, 1, keepdims=False).astype(BF)
    part_two = exchange(part_two, ALL, plane_groups(hosts, devs))
    sum_two = jnp.sum(part_two.astype(F32), 0)

    back_self = lax.dot_general(
        cotangent, w_self2, (((1,), (1,)), ((), ())), preferred_element_type=F32
    )
    back_mean = (
        lax.dot_general(cotangent, w_nbr2, (((1,), (1,)), ((), ())), preferred_element_type=F32)
        / seed_float
    )
    seat = jnp.arange(FAN1, dtype=jnp.int32)[None, :] < seed_counts[:, None]
    back_hop = back_mean[:, None, :] * seat.astype(F32)[:, :, None]
    back = jnp.concatenate([back_self, back_hop.reshape(seeds * FAN1, hidden)], 0)
    back_pre = (back * gate * (1.0 + pre * (1.0 - gate))).astype(BF)

    rows_one = jnp.concatenate([own, mean_one], 1)
    part_one = lax.dot_general(
        back_pre, rows_one, (((0,), (0,)), ((), ())), preferred_element_type=F32
    )
    part_one = part_one.reshape(count // 2, 2, cols, 2 * width)
    give = lax.dynamic_index_in_dim(part_one, 1 - core, 1, keepdims=False).astype(BF)
    keep = lax.dynamic_index_in_dim(part_one, core, 1, keepdims=False)
    part_one = (keep + swap_pair(give, devs).astype(F32)).astype(BF)
    part_one = exchange(part_one, ALL, parity_groups(hosts, devs))
    sum_one = jnp.sum(part_one.astype(F32), 0)
    return (
        embedding,
        moved[None],
        sum_one[:, :width].T,
        sum_one[:, width:].T,
        sum_two[:, :hidden].T,
        sum_two[:, hidden:].T,
    )


def solution(mesh):
    return jax.shard_map(
        local,
        mesh=mesh,
        in_specs=(
            P(ALL, None), P("hst", "dev", None), P("hst", "dev"), P(ALL, None, None, None),
            P(ALL, None, None), P(ALL), P(ALL, None), P(ALL), P(ALL), P(), P(), P(), P(),
            P(ALL, None),
        ),
        out_specs=(
            P(ALL, None), P("hst", "dev", None), P(None, ALL), P(None, ALL), P(None, ALL),
            P(None, ALL),
        ),
        check_vma=False,
    )
```

```python
import functools

import jax
import jax.numpy as jnp
from jax import lax
from jax.experimental import pallas as pl
from jax.experimental.pallas import tpu as pltpu
from jax.sharding import PartitionSpec as P


FAN1 = 25
FAN2 = 15
CSLOT = 2
BLOCK = 128
ALL = ("hst", "dev")
BF = jnp.bfloat16
F32 = jnp.float32


def parity_groups(hosts, devs):
    return [
        [h * devs + 2 * i + c for h in range(hosts) for i in range(devs // 2)] for c in range(2)
    ]


def exchange(x, axes, groups=None):
    return lax.all_to_all(
        x, axes, split_axis=0, concat_axis=0, tiled=True, axis_index_groups=groups
    )


def swap_pair(x, devs):
    return lax.ppermute(x, "dev", [(i, i ^ 1) for i in range(devs)])


def along_z(x, k, hosts):
    return lax.ppermute(x, "hst", [(i, (i + k) % hosts) for i in range(hosts)])


def call(body, outs, cost, *args, near=(), far=(), scratch=(), limit=8):
    space = pl.BlockSpec(memory_space=pltpu.VMEM)
    scalar = pl.BlockSpec(memory_space=pltpu.SMEM)
    away = pl.BlockSpec(memory_space=pl.ANY)
    flops, traffic = cost
    kinds = [scalar if x.ndim == 1 else away if i in far else space for i, x in enumerate(args)]
    args = [
        pltpu.with_memory_space_constraint(x, pltpu.VMEM) if i in near else x
        for i, x in enumerate(args)
    ]
    return pl.pallas_call(
        body,
        out_shape=outs,
        in_specs=kinds,
        out_specs=jax.tree.map(lambda _: space, outs),
        scratch_shapes=scratch,
        cost_estimate=pl.CostEstimate(flops=flops, transcendentals=0, bytes_accessed=traffic),
        compiler_params=pltpu.CompilerParams(vmem_limit_bytes=limit << 20),
    )(*args)


def product(a, b):
    return jnp.dot(a, b, preferred_element_type=F32)


def across(a, b):
    return lax.dot_general(a, b, (((0,), (0,)), ((), ())), preferred_element_type=F32)


def along(a, b):
    return lax.dot_general(a, b, (((1,), (1,)), ((), ())), preferred_element_type=F32)


def serve(asked_ref, stored_ref, got_ref, out_hbm, out_ref, sems, *, rows_dev, sub, tile):
    span = got_ref.shape[0] // 2
    half = got_ref.shape[1]
    block = span // CSLOT
    ones = jnp.ones((span, 128), BF)
    copies = []
    for t in range(stored_ref.shape[0] // tile):
        rows = slice(t * tile, (t + 1) * tile)
        row = asked_ref[:, rows] - rows_dev
        inner = row % block
        place = (inner // sub) * (CSLOT * sub) + (row // block) * sub + inner % sub
        place = jnp.where(row >= 0, place, -1)
        pick = (place == lax.broadcasted_iota(jnp.int32, (span, tile), 0)).astype(F32)
        pick = pick.astype(BF)
        hit = across(pick, ones) > 0.5
        for j in range(2):
            cached = across(pick, got_ref[j * span : (j + 1) * span, :])
            for i in range(half // 128):
                cols = slice(j * half + i * 128, j * half + (i + 1) * 128)
                stored = stored_ref[rows, cols].astype(F32)
                cell = jnp.where(hit, cached[:, i * 128 : (i + 1) * 128], stored)
                out_ref[rows, cols] = cell.astype(BF)
        copies.append(
            pltpu.make_async_copy(
                out_ref.at[pl.ds(t * tile, tile), :], out_hbm.at[pl.ds(t * tile, tile), :], sems.at[t]
            )
        )
        copies[-1].start()
    for copy in copies:
        copy.wait()


def serve_all(asked, stored, got, rows_dev, sub, tile):
    slots, width = stored.shape
    space = pl.BlockSpec(memory_space=pltpu.VMEM)
    return pl.pallas_call(
        functools.partial(serve, rows_dev=rows_dev, sub=sub, tile=tile),
        out_shape=pltpu.HBM((slots, width), BF),
        in_specs=[space] * 3,
        out_specs=pl.BlockSpec(memory_space=pltpu.HBM),
        scratch_shapes=[pltpu.VMEM((slots, width), BF), pltpu.SemaphoreType.DMA((slots // tile,))],
        cost_estimate=pl.CostEstimate(
            flops=slots * got.shape[0] * width, transcendentals=0, bytes_accessed=4 * slots * width
        ),
        compiler_params=pltpu.CompilerParams(vmem_limit_bytes=16 << 20),
    )(asked, pltpu.with_memory_space_constraint(stored, pltpu.VMEM), got)


def sort(host_ref, got_ref, *out_refs, sub):
    devs, _, half = got_ref.shape
    hosts = len(out_refs) - 1
    rows = devs * CSLOT * sub
    note = got_ref[:, CSLOT * sub :, :128].astype(F32)
    block = jnp.concatenate(
        [
            jnp.broadcast_to(note[:, :, 64 + j : 65 + j], (devs, sub, 128)).reshape(devs, 1, sub, 128)
            for j in range(CSLOT)
        ],
        1,
    ).reshape(rows, 128)
    inner = lax.broadcasted_iota(jnp.int32, (rows, 128), 0) % sub
    source = block.astype(jnp.int32) * sub + inner
    lane = lax.broadcasted_iota(jnp.int32, (rows, 128), 1)
    pick = jnp.concatenate(
        [(source == lane + i * 128).astype(F32) for i in range(rows // 128)], 1
    ).astype(BF)
    pieces = got_ref[:, : CSLOT * sub, :].reshape(rows, half)
    out_refs[0][...] = product(pick, pieces).astype(BF)
    for k in range(hosts):
        host = (host_ref[0] + k) % hosts
        line = lax.broadcasted_iota(jnp.int32, note.shape, 1)
        out_refs[1 + k][...] = jnp.sum(jnp.where(line == host, note, 0.0), 1).astype(BF)


def decode(host_ref, *refs, cap, top):
    parts, (asked_ref, stored_ref) = refs[:-2], refs[-2:]
    hosts = len(parts)
    devs = parts[0].shape[0]
    span = devs * cap
    lane = lax.broadcasted_iota(jnp.int32, (devs, span), 1)
    spread = (lane // cap == lax.broadcasted_iota(jnp.int32, (devs, span), 0)).astype(F32)
    spread = spread.astype(BF)
    line = lax.broadcasted_iota(jnp.int32, (128, span), 0)
    place = lax.broadcasted_iota(jnp.int32, (128, span), 1) % cap
    scale = jnp.where(line == place, 256.0, jnp.where(line == place + cap, 1.0, 0.0))
    rows = [
        jnp.sum(across(p[...], spread) * scale, 0, keepdims=True).astype(jnp.int32) for p in parts
    ]
    for j in range(hosts):
        turn = (host_ref[0] - j + hosts) % hosts
        row = jnp.zeros((1, span), jnp.int32)
        for k in range(hosts):
            row = jnp.where(turn == k, rows[k], row)
        asked_ref[:, j * span : (j + 1) * span] = row
        stored_ref[:, j * span : (j + 1) * span] = jnp.minimum(row, top)


def mark(near_ref, self_ref, hop_ref, count_ref, one_ref, many_ref, share_ref, used_ref,
         table_ref, *, tile, cap):
    nodes, slots = one_ref.shape
    peers = count_ref.shape[1]
    lane = lax.broadcasted_iota(jnp.int32, (peers, slots), 1)
    spread = lane // cap == lax.broadcasted_iota(jnp.int32, (peers, slots), 0)
    counts = jnp.broadcast_to(count_ref[...].astype(F32), (16, peers)).astype(BF)
    counts = product(counts, spread.astype(F32).astype(BF))
    rank = lax.broadcasted_iota(jnp.int32, counts.shape, 1) % cap
    used_ref[...] = (rank.astype(F32) < counts).astype(F32).astype(BF)

    hop = hop_ref[...]
    near = near_ref[...]
    near = jnp.where(lax.broadcasted_iota(jnp.int32, near.shape, 0) < hop, near, slots)
    rows = jnp.concatenate([near, self_ref[...]], 0)
    high = (rows // 256).astype(F32).astype(BF)
    low = (rows % 256).astype(F32).astype(BF)
    lines = rows.shape[0]
    turn = lax.broadcasted_iota(jnp.int32, (lines, 128), 0)
    turn = (turn == lax.broadcasted_iota(jnp.int32, (lines, 128), 1)).astype(F32).astype(BF)
    table_ref[...] = (256.0 * across(high, turn) + across(low, turn)).astype(jnp.int32)
    all_hop = jnp.broadcast_to(hop.astype(F32), (16, nodes)).astype(BF)
    first = lax.broadcasted_iota(jnp.int32, (16, 128), 0) == 0
    share_ref[...] = 1.0 / across(all_hop, first.astype(F32).astype(BF))
    kind = jnp.int16

    def step(i, carry):
        rows = pl.ds(i * tile, tile)
        table = table_ref[rows, :]
        named = [
            jnp.broadcast_to(table[:, k : k + 1], (tile, 128)).astype(kind)
            for k in range(FAN2 + 1)
        ]
        lane = lax.broadcasted_iota(jnp.int32, (tile, 128), 1)
        yes, no = jnp.ones((tile, 128), BF), jnp.zeros((tile, 128), BF)
        for j in range(slots // 128):
            cols = slice(j * 128, (j + 1) * 128)
            slot = (lane + j * 128).astype(kind)
            live = used_ref[:, cols]
            one_ref[rows, cols] = jnp.where(named[FAN2] == slot, yes, no) * live
            total = jnp.where(named[0] == slot, yes, no)
            for k in range(1, FAN2):
                total = total + jnp.where(named[k] == slot, yes, no)
            many_ref[rows, cols] = total * live
        return carry

    lax.fori_loop(0, nodes // tile, step, 0)


def ready(core_ref, self1_ref, nbr1_ref, order_ref, weight_ref, *, cols):
    width = self1_ref.shape[0]
    hidden = order_ref.shape[0]
    pos = lax.broadcasted_iota(jnp.int32, (1, hidden), 1)
    inner = pos % (hidden // 2)
    side = jnp.where(pos < hidden // 2, 1 - core_ref[0], core_ref[0])
    source = (inner // cols) * (2 * cols) + side * cols + inner % cols
    hot = source == lax.broadcasted_iota(jnp.int32, (hidden, hidden), 0)
    order_ref[...] = hot.astype(F32).astype(BF)
    weight_ref[:width, :] = product(self1_ref[...], order_ref[...]).astype(BF)
    weight_ref[width:, :] = product(nbr1_ref[...], order_ref[...]).astype(BF)


def spread_back(order_ref, self2_ref, nbr2_ref, col_ref, row_ref, cot_ref, *refs):
    others, (back_ref, turned_ref) = refs[:-2], refs[-2:]
    rows = jnp.concatenate([cot_ref[...]] + [r[...] for r in others], 0)
    turned_ref[...] = product(rows, order_ref[...]).astype(BF)
    seeds = cot_ref.shape[0]
    nodes = back_ref.shape[0]
    back_self = along(cot_ref[...], self2_ref[...])
    back_mean = along(cot_ref[...], nbr2_ref[...]) / col_ref[...].astype(F32)
    rest = jnp.concatenate([back_self, back_mean], 0)
    pieces = []
    for _ in range(3):
        piece = rest.astype(BF)
        rest = rest - piece.astype(F32)
        pieces.append(piece)
    lane = lax.broadcasted_iota(jnp.int32, (1, 6 * seeds), 1) % (2 * seeds)
    seed = lane % seeds
    first = jnp.where(lane < seeds, seed, seeds + seed * FAN1)
    last = jnp.where(lane < seeds, seed + 1, first + row_ref[...])
    node = lax.broadcasted_iota(jnp.int32, (nodes, 6 * seeds), 0)
    spread = ((node >= first) & (node < last)).astype(F32).astype(BF)
    pieces = product(jnp.concatenate(pieces, 0), order_ref[...]).astype(BF)
    back_ref[...] = product(spread, pieces)


def layer(host_ref, fetched_hbm, one_hbm, many_hbm, weight_hbm, back_hbm, order_hbm, share_ref, col_ref,
          rows_ref, grad_ref, pair_ref, part0_ref, part1_ref, part2_ref, part3_ref,
          fetched_ref, one_ref, many_ref, weight_ref, back_ref, order_ref, hid_ref, sems, *, tile):
    away = (fetched_hbm, one_hbm, many_hbm, weight_hbm, back_hbm, order_hbm)
    held = (fetched_ref, one_ref, many_ref, weight_ref, back_ref, order_ref)
    loads = [pltpu.make_async_copy(a, b, sems.at[i]) for i, (a, b) in enumerate(zip(away, held))]
    for load in loads:
        load.start()
    nodes = one_ref.shape[0]
    width = fetched_ref.shape[1]
    seeds = col_ref.shape[0]
    hidden = weight_ref.shape[1]
    loads[0].wait()
    loads[1].wait()
    for i in range(nodes // tile):
        rows = slice(i * tile, (i + 1) * tile)
        rows_ref[rows, :width] = product(one_ref[rows, :], fetched_ref[...]).astype(BF)
        if i == 0:
            loads[2].wait()
        total = product(many_ref[rows, :], fetched_ref[...])
        rows_ref[rows, width:] = (total * share_ref[rows, :1]).astype(BF)
        if i == 0:
            loads[3].wait()
            loads[4].wait()
        pre = product(rows_ref[rows, :], weight_ref[...])
        gate = 1.0 / (1.0 + jnp.exp(-pre))
        hid_ref[rows, :] = (pre * gate).astype(BF)
        grad_ref[rows, :] = (back_ref[rows, :] * gate * (1.0 + pre * (1.0 - gate))).astype(BF)
    loads[5].wait()
    node = lax.broadcasted_iota(jnp.int32, (seeds, nodes), 1)
    first = seeds + lax.broadcasted_iota(jnp.int32, (seeds, nodes), 0) * FAN1
    live = ((node >= first) & (node < first + col_ref[...])).astype(F32).astype(BF)
    mean = (product(live, hid_ref[...]) / col_ref[...].astype(F32)).astype(BF)
    pair_ref[:, :hidden] = along(hid_ref[:seeds, :], order_ref[...]).astype(BF)
    pair_ref[:, hidden:] = along(mean, order_ref[...]).astype(BF)
    parts = (part0_ref, part1_ref, part2_ref, part3_ref)
    slab = hidden // len(parts)
    for k in range(len(parts)):
        start = pl.multiple_of((host_ref[0] + k) % len(parts) * slab, slab)
        parts[k][:, :slab] = pair_ref[:, pl.ds(start, slab)]
        parts[k][:, slab:] = pair_ref[:, pl.ds(hidden + start, slab)]


def give_one(grad_ref, rows_ref, give_ref):
    hidden = grad_ref.shape[1]
    give_ref[...] = across(grad_ref[:, : hidden // 2], rows_ref[...]).astype(BF)


def give_two(cot_ref, *refs):
    parts, give_ref = refs[:-1], refs[-1]
    rows = jnp.concatenate([p[...] for p in parts], 0)
    give_ref[...] = across(cot_ref[:, : cot_ref.shape[1] // 2], rows).astype(BF)


def stay(grad_ref, rows_ref, taken_ref, cot_ref, taken2_ref, *refs):
    parts, out_ref = refs[:-1], refs[-1]
    half = grad_ref.shape[1] // 2
    wide = rows_ref.shape[1]
    kept = across(grad_ref[:, half:], rows_ref[...])
    out_ref[:, :wide] = (kept + taken_ref[...].astype(F32)).astype(BF)
    rows = jnp.concatenate([p[...] for p in parts], 0)
    kept = across(cot_ref[:, half:], rows)
    out_ref[:, wide:] = (kept + taken2_ref[...].astype(F32)).astype(BF)


def step(
    features, cache_blocks, plan, miss_ids, miss_counts, self_ids, nbr_ids, hop_counts,
    seed_counts, w_self1, w_nbr1, w_self2, w_nbr2, cotangent,
):
    hosts = lax.axis_size("hst")
    devs = lax.axis_size("dev")
    count = hosts * devs
    rows_dev, width = features.shape
    hidden = w_self2.shape[0]
    cap = miss_ids.shape[3]
    nodes = self_ids.shape[0]
    seeds = seed_counts.shape[0]
    h = lax.axis_index("hst")
    d = lax.axis_index("dev")
    core = d % 2
    half = width // 2
    groups = devs // 2
    sub = BLOCK // groups
    slots = count * cap
    cols = hidden // count
    shape = jax.ShapeDtypeStruct

    pieces = cache_blocks.reshape(CSLOT, groups, sub, 2, half).transpose(3, 1, 0, 2, 4)
    pieces = pieces.reshape(devs, CSLOT * sub, half)
    ids = miss_ids[0].transpose(1, 0, 2)
    ids = jnp.concatenate([ids // 256, ids % 256], 2)
    ids = jnp.pad(ids, ((0, 0), (0, 0), (0, half - 2 * cap)))
    own_plan = jnp.pad(plan[:, None, :], ((0, 0), (0, 0), (64, half - 64 - CSLOT)))
    ids = jnp.pad(ids, ((0, 0), (0, sub - hosts), (0, 0)))
    note = (ids + own_plan).astype(BF)
    got = exchange(jnp.concatenate([pieces, note], 1), "dev")

    cots = [cotangent] + [along_z(cotangent, k, hosts) for k in range(1, hosts)]
    got, cots = lax.optimization_barrier((got, cots))

    line = shape((devs, 128), BF)
    pieces, *parts = call(
        functools.partial(sort, sub=sub),
        (shape((devs * CSLOT * sub, half), BF),) + (line,) * hosts,
        (2 * devs * devs * CSLOT * CSLOT * sub * sub * half, 8 * devs * half),
        h[None], got,
    )
    for k in range(1, hosts):
        parts[k] = along_z(parts[k], k, hosts)
    pieces = exchange(pieces.reshape(devs, CSLOT * sub, half), "dev")
    moved = (
        pieces.reshape(2, groups, CSLOT, sub, half)
        .transpose(2, 1, 3, 0, 4)
        .reshape(CSLOT * BLOCK, width)
    )

    asked, kept = call(
        functools.partial(decode, cap=cap, top=rows_dev - 1),
        (shape((1, slots), jnp.int32), shape((1, slots), jnp.int32)),
        (slots * devs * 256, 64 * slots), h[None], *parts,
    )
    stored = features.at[kept.reshape(slots)].get(mode="promise_in_bounds")
    served = serve_all(
        asked, stored, pieces.reshape(2 * CSLOT * BLOCK, half), rows_dev, sub, 512
    )
    fetched = exchange(served.reshape(count, cap, width), ALL).reshape(slots, width)

    reordered, weight = call(
        functools.partial(ready, cols=cols),
        (pltpu.HBM((hidden, hidden), BF), pltpu.HBM((2 * width, hidden), BF)),
        (4 * width * hidden * hidden, 12 * hidden * hidden),
        core[None], w_self1, w_nbr1, limit=24,
    )
    one, many, share = call(
        functools.partial(mark, tile=16, cap=cap),
        (pltpu.HBM((nodes, slots), BF), pltpu.HBM((nodes, slots), BF), pltpu.HBM((nodes, 128), F32)),
        (nodes * slots * 48, 4 * nodes * slots),
        nbr_ids.T, self_ids[None], hop_counts[None], miss_counts.reshape(1, count), limit=24,
        scratch=[pltpu.VMEM((16, slots), BF), pltpu.VMEM((nodes, 128), jnp.int32)],
    )
    back, turned = call(
        spread_back,
        (pltpu.HBM((nodes, hidden), F32), pltpu.HBM((hosts * seeds, hidden), BF)),
        (8 * seeds * hidden * hidden, 12 * hidden * hidden),
        reordered, w_self2, w_nbr2, seed_counts[:, None], jnp.tile(seed_counts, 6)[None], *cots,
        limit=24,
    )

    held = (fetched, one, many, weight, back, reordered)
    part = shape((seeds, 2 * hidden // hosts), BF)
    rows_one, grad, both, *parts = call(
        functools.partial(layer, tile=nodes // 2),
        (
            pltpu.VMEM((nodes, 2 * width), BF), pltpu.VMEM((nodes, hidden), BF),
            shape((seeds, 2 * hidden), BF), part, part, part, part,
        ),
        (4 * nodes * slots * width, 8 * nodes * slots),
        h[None], *held, share, seed_counts[:, None],
        far=tuple(range(1, 1 + len(held))), limit=40,
        scratch=[pltpu.VMEM(x.shape, x.dtype) for x in held]
        + [pltpu.VMEM((nodes, hidden), BF), pltpu.SemaphoreType.DMA((len(held),))],
    )

    parts = parts[:1] + [along_z(parts[k], k, hosts) for k in range(1, hosts)]
    give = call(
        give_one, shape((hidden // 2, 2 * width), BF),
        (2 * nodes * hidden * width, 4 * hidden * width), grad, rows_one,
        near=(0, 1), limit=16,
    )
    taken = swap_pair(give, devs)
    give = call(
        give_two, shape((hidden // 2, 2 * hidden // hosts), BF),
        (4 * hidden * hidden * seeds, hidden * hidden), turned, *parts,
    )
    taken_two = swap_pair(give, devs)
    tall = 2 * width + 2 * hidden // hosts
    part = call(
        stay, shape((hidden // 2, tall), BF),
        (2 * nodes * hidden * width, 4 * hidden * width), grad, rows_one, taken, turned, taken_two,
        *parts, near=(0, 1), limit=24,
    )
    part = exchange(part.reshape(count // 2, cols, tall), ALL, parity_groups(hosts, devs))

    embedding = (product(both[:, :hidden], w_self2) + product(both[:, hidden:], w_nbr2)).astype(BF)
    sum_one = jnp.sum(part[:, :, : 2 * width].astype(F32), 0)
    sum_two = part[:, :, 2 * width :].reshape(hosts, groups, cols, 2, hidden // hosts)
    sum_two = jnp.sum(sum_two.astype(F32), 1).transpose(2, 1, 0, 3).reshape(2, cols, hidden)
    return (
        embedding,
        moved[None],
        sum_one[:, :width].T,
        sum_one[:, width:].T,
        sum_two[0].T,
        sum_two[1].T,
    )


def solution(mesh):
    return jax.shard_map(
        step,
        mesh=mesh,
        in_specs=(
            P(ALL, None), P("hst", "dev", None), P("hst", "dev"), P(ALL, None, None, None),
            P(ALL, None, None), P(ALL), P(ALL, None), P(ALL), P(ALL), P(), P(), P(), P(),
            P(ALL, None),
        ),
        out_specs=(
            P(ALL, None), P("hst", "dev", None), P(None, ALL), P(None, ALL), P(None, ALL),
            P(None, ALL),
        ),
        check_vma=False,
    )
```

```python
import functools

import jax
import jax.numpy as jnp
from jax import lax
from jax.experimental import pallas as pl
from jax.experimental.pallas import tpu as pltpu
from jax.sharding import PartitionSpec as P


FAN1 = 25
FAN2 = 15
CSLOT = 2
BLOCK = 128
ALL = ("hst", "dev")
BF = jnp.bfloat16
F32 = jnp.float32


def parity_groups(hosts, devs):
    return [
        [h * devs + 2 * i + c for h in range(hosts) for i in range(devs // 2)] for c in range(2)
    ]


def exchange(x, axes, groups=None):
    return lax.all_to_all(
        x, axes, split_axis=0, concat_axis=0, tiled=True, axis_index_groups=groups
    )


def swap_pair(x, devs):
    return lax.ppermute(x, "dev", [(i, i ^ 1) for i in range(devs)])


def along_z(x, k, hosts):
    return lax.ppermute(x, "hst", [(i, (i + k) % hosts) for i in range(hosts)])


class Left:
    def __init__(self, shape, kind):
        self.ref = pltpu.HBM(shape, kind)


def is_left(x):
    return isinstance(x, Left)


def call(body, outs, cost, *args, near=(), far=(), scratch=(), limit=8):
    space = pl.BlockSpec(memory_space=pltpu.VMEM)
    scalar = pl.BlockSpec(memory_space=pltpu.SMEM)
    away = pl.BlockSpec(memory_space=pltpu.HBM)
    flops, traffic = cost
    kinds = [scalar if x.ndim == 1 else away if i in far else space for i, x in enumerate(args)]
    place = {**{i: pltpu.VMEM for i in near}, **{i: pltpu.HBM for i in far}}
    args = [
        pltpu.with_memory_space_constraint(x, place[i]) if i in place else x
        for i, x in enumerate(args)
    ]
    left = [isinstance(x, Left) for x in jax.tree.leaves(outs, is_leaf=is_left)]
    outs = jax.tree.map(lambda x: x.ref if is_left(x) else x, outs, is_leaf=is_left)
    tree = jax.tree.structure(outs)
    return pl.pallas_call(
        body,
        out_shape=outs,
        in_specs=kinds,
        out_specs=jax.tree.unflatten(tree, [away if x else space for x in left]),
        scratch_shapes=scratch,
        cost_estimate=pl.CostEstimate(flops=flops, transcendentals=0, bytes_accessed=traffic),
        compiler_params=pltpu.CompilerParams(vmem_limit_bytes=limit << 20),
    )(*args)


def product(a, b):
    return jnp.dot(a, b, preferred_element_type=F32)


def across(a, b):
    return lax.dot_general(a, b, (((0,), (0,)), ((), ())), preferred_element_type=F32)


def along(a, b):
    return lax.dot_general(a, b, (((1,), (1,)), ((), ())), preferred_element_type=F32)


def pack(plan_ref, ids_hbm, block_hbm, out_ref, ids_ref, block_ref, sems, *, sub):
    devs, _, _ = out_ref.shape
    groups = devs // 2
    half = block_ref.shape[1] // 2
    load_ids = pltpu.make_async_copy(ids_hbm, ids_ref, sems.at[0])
    load_block = pltpu.make_async_copy(block_hbm, block_ref, sems.at[1])
    load_ids.start()
    load_block.start()
    load_ids.wait()
    hosts, cap, _ = ids_ref.shape
    line = lax.broadcasted_iota(jnp.int32, (cap, 128), 0)
    lane = lax.broadcasted_iota(jnp.int32, (cap, 128), 1)
    to_high = (lane == line).astype(F32).astype(BF)
    to_low = (lane == line + cap).astype(F32).astype(BF)
    row = lax.broadcasted_iota(jnp.int32, (devs, sub, 128), 1)
    lane = lax.broadcasted_iota(jnp.int32, (devs, sub, 128), 2)
    note = jnp.zeros((devs, sub, 128), F32)
    for k in range(hosts):
        ids = ids_ref[k]
        high = (ids // 256).astype(F32).astype(BF)
        low = (ids % 256).astype(F32).astype(BF)
        part = across(high, to_high) + across(low, to_low)
        note = jnp.where(row == k, part[:, None, :], note)
    for j in range(CSLOT):
        note = jnp.where(lane == 64 + j, plan_ref[j].astype(F32), note)
    out_ref[:, :, CSLOT * half :] = note.astype(BF)
    load_block.wait()
    block = block_ref[...].astype(F32).reshape(CSLOT, groups, sub, 2 * half)
    for j in range(2):
        for i in range(CSLOT):
            piece = block[i, :, :, j * half : (j + 1) * half].astype(BF)
            out_ref[j * groups : (j + 1) * groups, :, i * half : (i + 1) * half] = piece


def serve(asked_ref, got_ref, stored_hbm, out_hbm, stored_ref, out_ref, in_sems, out_sems, *,
          rows_dev, sub, tile):
    steps = stored_ref.shape[0] // tile
    span = got_ref.shape[0] // 2
    half = got_ref.shape[1]
    block = span // CSLOT
    ones = jnp.ones((span, 128), BF)
    chunks = [pl.ds(t * tile, tile) for t in range(steps)]
    loads = [
        pltpu.make_async_copy(stored_hbm.at[c, :], stored_ref.at[c, :], in_sems.at[t])
        for t, c in enumerate(chunks)
    ]
    stores = [
        pltpu.make_async_copy(out_ref.at[c, :], out_hbm.at[c, :], out_sems.at[t])
        for t, c in enumerate(chunks)
    ]
    for load in loads:
        load.start()
    for t in range(steps):
        rows = slice(t * tile, (t + 1) * tile)
        row = asked_ref[:, rows] - rows_dev
        inner = row % block
        place = (inner // sub) * (CSLOT * sub) + (row // block) * sub + inner % sub
        place = jnp.where(row >= 0, place, -1)
        pick = (place == lax.broadcasted_iota(jnp.int32, (span, tile), 0)).astype(F32)
        pick = pick.astype(BF)
        hit = across(pick, ones) > 0.5
        cached = [across(pick, got_ref[j * span : (j + 1) * span, :]) for j in range(2)]
        loads[t].wait()
        for j in range(2):
            for i in range(half // 128):
                cols = slice(j * half + i * 128, j * half + (i + 1) * 128)
                stored = stored_ref[rows, cols].astype(F32)
                cell = jnp.where(hit, cached[j][:, i * 128 : (i + 1) * 128], stored)
                out_ref[rows, cols] = cell.astype(BF)
        stores[t].start()
    for store in stores:
        store.wait()


def sort(host_ref, got_ref, pieces_ref, *part_refs, sub):
    devs, _, tall = got_ref.shape
    hosts = len(part_refs)
    half = (tall - 128) // CSLOT
    rows = devs * CSLOT * sub
    note = got_ref[:, :, CSLOT * half :].astype(F32)
    block = jnp.concatenate(
        [
            jnp.broadcast_to(note[:, :, 64 + j : 65 + j], (devs, sub, 128)).reshape(devs, 1, sub, 128)
            for j in range(CSLOT)
        ],
        1,
    ).reshape(rows, 128)
    block = block.astype(jnp.int32)
    inner = lax.broadcasted_iota(jnp.int32, (rows, 128), 0) % sub
    lane = lax.broadcasted_iota(jnp.int32, (rows, 128), 1)
    total = jnp.zeros((rows, half), F32)
    for j in range(CSLOT):
        source = jnp.where(block % CSLOT == j, block // CSLOT * sub + inner, -1)
        pick = jnp.concatenate(
            [(source == lane + i * 128).astype(F32) for i in range(devs * sub // 128)], 1
        ).astype(BF)
        piece = got_ref[:, :, j * half : (j + 1) * half].astype(F32).reshape(devs * sub, half)
        total = total + product(pick, piece.astype(BF))
    pieces_ref[...] = total.astype(BF)
    line = lax.broadcasted_iota(jnp.int32, note.shape, 1)
    for k in range(hosts):
        host = (host_ref[0] + k) % hosts
        part_refs[k][...] = jnp.sum(jnp.where(line == host, note, 0.0), 1).astype(BF)


def decode(host_ref, *refs, cap, top):
    parts, (asked_ref, stored_ref) = refs[:-2], refs[-2:]
    hosts = len(parts)
    devs = parts[0].shape[0]
    span = devs * cap
    lane = lax.broadcasted_iota(jnp.int32, (devs, span), 1)
    spread = (lane // cap == lax.broadcasted_iota(jnp.int32, (devs, span), 0)).astype(F32)
    spread = spread.astype(BF)
    line = lax.broadcasted_iota(jnp.int32, (128, span), 0)
    place = lax.broadcasted_iota(jnp.int32, (128, span), 1) % cap
    scale = jnp.where(line == place, 256.0, jnp.where(line == place + cap, 1.0, 0.0))
    found = []
    for part in parts:
        ids = across(part[...], spread) * scale
        found.append(jnp.sum(ids, 0, keepdims=True).astype(jnp.int32))
    for j in range(hosts):
        turn = (host_ref[0] - j + hosts) % hosts
        row = found[0]
        for k in range(1, hosts):
            row = jnp.where(turn == k, found[k], row)
        asked_ref[:, j * span : (j + 1) * span] = row
        stored_ref[:, j * span : (j + 1) * span] = jnp.minimum(row, top)


def mark(near_ref, self_ref, hop_ref, count_ref, one_ref, many_ref, share_ref, used_ref,
         table_ref, *, tile, cap):
    nodes, slots = one_ref.shape
    peers = count_ref.shape[1]
    lane = lax.broadcasted_iota(jnp.int32, (peers, slots), 1)
    spread = lane // cap == lax.broadcasted_iota(jnp.int32, (peers, slots), 0)
    counts = jnp.broadcast_to(count_ref[...].astype(F32), (16, peers)).astype(BF)
    counts = product(counts, spread.astype(F32).astype(BF))
    rank = lax.broadcasted_iota(jnp.int32, counts.shape, 1) % cap
    used_ref[...] = (rank.astype(F32) < counts).astype(F32).astype(BF)

    hop = hop_ref[...]
    near = near_ref[...]
    near = jnp.where(lax.broadcasted_iota(jnp.int32, near.shape, 0) < hop, near, slots)
    rows = jnp.concatenate([near, self_ref[...]], 0)
    high = (rows // 256).astype(F32).astype(BF)
    low = (rows % 256).astype(F32).astype(BF)
    lines = rows.shape[0]
    turn = lax.broadcasted_iota(jnp.int32, (lines, 128), 0)
    turn = (turn == lax.broadcasted_iota(jnp.int32, (lines, 128), 1)).astype(F32).astype(BF)
    table_ref[...] = (256.0 * across(high, turn) + across(low, turn)).astype(jnp.int32)
    all_hop = jnp.broadcast_to(hop.astype(F32), (16, nodes)).astype(BF)
    first = lax.broadcasted_iota(jnp.int32, (16, 128), 0) == 0
    share_ref[...] = 1.0 / across(all_hop, first.astype(F32).astype(BF))
    kind = jnp.int16

    def step(i, carry):
        rows = pl.ds(i * tile, tile)
        table = table_ref[rows, :]
        named = [
            jnp.broadcast_to(table[:, k : k + 1], (tile, 128)).astype(kind)
            for k in range(FAN2 + 1)
        ]
        lane = lax.broadcasted_iota(jnp.int32, (tile, 128), 1)
        yes, no = jnp.ones((tile, 128), BF), jnp.zeros((tile, 128), BF)
        for j in range(slots // 128):
            cols = slice(j * 128, (j + 1) * 128)
            slot = (lane + j * 128).astype(kind)
            live = used_ref[:, cols]
            one_ref[rows, cols] = jnp.where(named[FAN2] == slot, yes, no) * live
            total = jnp.where(named[0] == slot, yes, no)
            for k in range(1, FAN2):
                total = total + jnp.where(named[k] == slot, yes, no)
            many_ref[rows, cols] = total * live
        return carry

    lax.fori_loop(0, nodes // tile, step, 0)


def ready(core_ref, self1_ref, nbr1_ref, order_ref, natural_ref, weight_ref, *, cols):
    width = self1_ref.shape[0]
    hidden = order_ref.shape[0]
    pos = lax.broadcasted_iota(jnp.int32, (1, hidden), 1)
    inner = pos % (hidden // 2)
    side = jnp.where(pos < hidden // 2, 1 - core_ref[0], core_ref[0])
    source = (inner // cols) * (2 * cols) + side * cols + inner % cols
    hot = source == lax.broadcasted_iota(jnp.int32, (hidden, hidden), 0)
    order_ref[...] = hot.astype(F32).astype(BF)
    block = pos // cols
    place = jnp.where(block % 2 == core_ref[0], hidden // 2, 0) + block // 2 * cols + pos % cols
    hot = place == lax.broadcasted_iota(jnp.int32, (hidden, hidden), 0)
    natural_ref[...] = hot.astype(F32).astype(BF)
    weight_ref[:width, :] = product(self1_ref[...], order_ref[...]).astype(BF)
    weight_ref[width:, :] = product(nbr1_ref[...], order_ref[...]).astype(BF)


def spread_back(order_ref, self2_ref, nbr2_ref, col_ref, row_ref, cot_ref, *refs):
    others, (back_ref, turned_ref) = refs[:-2], refs[-2:]
    rows = jnp.concatenate([cot_ref[...]] + [r[...] for r in others], 0)
    turned_ref[...] = product(rows, order_ref[...]).astype(BF)
    seeds = cot_ref.shape[0]
    nodes = back_ref.shape[0]
    back_self = along(cot_ref[...], self2_ref[...])
    back_mean = along(cot_ref[...], nbr2_ref[...]) / col_ref[...].astype(F32)
    rest = jnp.concatenate([back_self, back_mean], 0)
    pieces = []
    for _ in range(3):
        piece = rest.astype(BF)
        rest = rest - piece.astype(F32)
        pieces.append(piece)
    lane = lax.broadcasted_iota(jnp.int32, (1, 6 * seeds), 1) % (2 * seeds)
    seed = lane % seeds
    first = jnp.where(lane < seeds, seed, seeds + seed * FAN1)
    last = jnp.where(lane < seeds, seed + 1, first + row_ref[...])
    node = lax.broadcasted_iota(jnp.int32, (nodes, 6 * seeds), 0)
    spread = ((node >= first) & (node < last)).astype(F32).astype(BF)
    pieces = product(jnp.concatenate(pieces, 0), order_ref[...]).astype(BF)
    back_ref[...] = product(spread, pieces)


def layer(host_ref, fetched_hbm, one_hbm, many_hbm, weight_hbm, back_hbm, natural_hbm, share_hbm, col_ref,
          rows_ref, grad_ref, pair_ref, part0_ref, part1_ref, part2_ref, part3_ref,
          fetched_ref, one_ref, many_ref, weight_ref, back_ref, natural_ref, share_ref, hid_ref, sems, *, tile):
    away = (fetched_hbm, one_hbm, many_hbm, weight_hbm, back_hbm, natural_hbm, share_hbm)
    held = (fetched_ref, one_ref, many_ref, weight_ref, back_ref, natural_ref, share_ref)
    loads = [pltpu.make_async_copy(a, b, sems.at[i]) for i, (a, b) in enumerate(zip(away, held))]
    for i in (0, 1, 2, 6, 3, 4, 5):
        loads[i].start()
    nodes = one_ref.shape[0]
    width = fetched_ref.shape[1]
    seeds = col_ref.shape[0]
    hidden = weight_ref.shape[1]
    loads[0].wait()
    loads[1].wait()
    for i in range(nodes // tile):
        rows = slice(i * tile, (i + 1) * tile)
        rows_ref[rows, :width] = product(one_ref[rows, :], fetched_ref[...]).astype(BF)
        if i == 0:
            loads[2].wait()
            loads[6].wait()
        total = product(many_ref[rows, :], fetched_ref[...])
        rows_ref[rows, width:] = (total * share_ref[rows, :1]).astype(BF)
        if i == 0:
            loads[3].wait()
            loads[4].wait()
        pre = product(rows_ref[rows, :], weight_ref[...])
        gate = 1.0 / (1.0 + jnp.exp(-pre))
        hid_ref[rows, :] = (pre * gate).astype(BF)
        grad_ref[rows, :] = (back_ref[rows, :] * gate * (1.0 + pre * (1.0 - gate))).astype(BF)
    loads[5].wait()
    node = lax.broadcasted_iota(jnp.int32, (seeds, nodes), 1)
    first = seeds + lax.broadcasted_iota(jnp.int32, (seeds, nodes), 0) * FAN1
    live = ((node >= first) & (node < first + col_ref[...])).astype(F32).astype(BF)
    mean = (product(live, hid_ref[...]) / col_ref[...].astype(F32)).astype(BF)
    both = product(jnp.concatenate([hid_ref[:seeds, :], mean], 0), natural_ref[...]).astype(BF)
    pair_ref[:, :hidden] = both[:seeds, :]
    pair_ref[:, hidden:] = both[seeds:, :]
    parts = (part0_ref, part1_ref, part2_ref, part3_ref)
    slab = hidden // len(parts)
    for k in range(len(parts)):
        start = pl.multiple_of((host_ref[0] + k) % len(parts) * slab, slab)
        parts[k][:, :slab] = pair_ref[:, pl.ds(start, slab)]
        parts[k][:, slab:] = pair_ref[:, pl.ds(hidden + start, slab)]


def give_one(grad_ref, rows_ref, give_ref):
    hidden = grad_ref.shape[1]
    give_ref[...] = across(grad_ref[:, : hidden // 2], rows_ref[...]).astype(BF)


def give_two(cot_ref, *refs):
    parts, give_ref = refs[:-1], refs[-1]
    rows = jnp.concatenate([p[...] for p in parts], 0)
    give_ref[...] = across(cot_ref[:, : cot_ref.shape[1] // 2], rows).astype(BF)


def stay(grad_ref, rows_ref, taken_ref, cot_ref, taken2_ref, *refs, steps):
    parts, (out_hbm, out_ref, sems) = refs[:-3], refs[-3:]
    half = grad_ref.shape[1] // 2
    wide = rows_ref.shape[1]
    rows = jnp.concatenate([p[...] for p in parts], 0)
    tile = half // steps
    stores = []
    for t in range(steps):
        cols = slice(half + t * tile, half + (t + 1) * tile)
        chunk = slice(t * tile, (t + 1) * tile)
        kept = across(grad_ref[:, cols], rows_ref[...])
        out_ref[chunk, :wide] = (kept + taken_ref[chunk, :].astype(F32)).astype(BF)
        kept = across(cot_ref[:, cols], rows)
        out_ref[chunk, wide:] = (kept + taken2_ref[chunk, :].astype(F32)).astype(BF)
        window = pl.ds(t * tile, tile)
        stores.append(
            pltpu.make_async_copy(out_ref.at[window, :], out_hbm.at[window, :], sems.at[t])
        )
        stores[-1].start()
    for store in stores:
        store.wait()


def total(part_hbm, self1_ref, nbr1_ref, self2_ref, nbr2_ref, part_ref, sems, *, hosts):
    sources = part_hbm.shape[0] // hosts
    width = self1_ref.shape[1]
    slab = self2_ref.shape[1] // hosts
    loads = []
    for i in range(hosts):
        window = pl.ds(i * sources, sources)
        loads.append(pltpu.make_async_copy(part_hbm.at[window], part_ref.at[window], sems.at[i]))
        loads[-1].start()
    for i in range(hosts):
        loads[i].wait()
        group = slice(i * sources, (i + 1) * sources)

        def add(start, size):
            return jnp.sum(part_ref[group, :, start : start + size].astype(F32), 0)

        if i == 0:
            self1_ref[...] = add(0, width)
            nbr1_ref[...] = add(width, width)
        else:
            self1_ref[...] += add(0, width)
            nbr1_ref[...] += add(width, width)
        cols = slice(i * slab, (i + 1) * slab)
        self2_ref[:, cols] = add(2 * width, slab)
        nbr2_ref[:, cols] = add(2 * width + slab, slab)


def step(
    features, cache_blocks, plan, miss_ids, miss_counts, self_ids, nbr_ids, hop_counts,
    seed_counts, w_self1, w_nbr1, w_self2, w_nbr2, cotangent,
):
    hosts = lax.axis_size("hst")
    devs = lax.axis_size("dev")
    count = hosts * devs
    rows_dev, width = features.shape
    hidden = w_self2.shape[0]
    cap = miss_ids.shape[3]
    nodes = self_ids.shape[0]
    seeds = seed_counts.shape[0]
    h = lax.axis_index("hst")
    d = lax.axis_index("dev")
    core = d % 2
    half = width // 2
    groups = devs // 2
    sub = BLOCK // groups
    slots = count * cap
    cols = hidden // count
    shape = jax.ShapeDtypeStruct

    tall = CSLOT * half + 128
    ids, block = miss_ids[0].transpose(0, 2, 1), cache_blocks[0]
    got = call(
        functools.partial(pack, sub=sub), pltpu.HBM((devs, sub, tall), BF),
        (16 * devs * sub * tall, 4 * devs * sub * tall), plan.reshape(CSLOT), ids, block,
        far=(1, 2),
        scratch=[pltpu.VMEM(x.shape, x.dtype) for x in (ids, block)]
        + [pltpu.SemaphoreType.DMA((2,))],
    )
    got = exchange(got, "dev")

    cots = [cotangent] + [along_z(cotangent, k, hosts) for k in range(1, hosts)]
    got, cots = lax.optimization_barrier((got, cots))

    line = shape((devs, 128), BF)
    pieces, *parts = call(
        functools.partial(sort, sub=sub),
        (pltpu.HBM((devs * CSLOT * sub, half), BF),) + (line,) * hosts,
        (2 * devs * devs * CSLOT * CSLOT * sub * sub * half, 8 * devs * half),
        h[None], got,
    )
    parts = parts[:1] + [along_z(parts[k], k, hosts) for k in range(1, hosts)]
    pieces = exchange(pieces.reshape(devs, CSLOT * sub, half), "dev")
    moved = (
        pieces.reshape(2, groups, CSLOT, sub, half)
        .transpose(2, 1, 3, 0, 4)
        .reshape(CSLOT * BLOCK, width)
    )

    line = shape((1, slots), jnp.int32)
    asked, kept = call(
        functools.partial(decode, cap=cap, top=rows_dev - 1), (line, line),
        (slots * devs * 256, 64 * slots), h[None], *parts,
    )
    stored = features.at[kept.reshape(slots)].get(mode="promise_in_bounds")
    tile = 256
    served = call(
        functools.partial(serve, rows_dev=rows_dev, sub=sub, tile=tile),
        Left((slots, width), BF), (4 * slots * CSLOT * BLOCK * width, 4 * slots * width),
        asked, pieces.reshape(2 * CSLOT * BLOCK, half), stored, far=(2,), limit=16,
        scratch=[pltpu.VMEM((slots, width), BF)] * 2
        + [pltpu.SemaphoreType.DMA((slots // tile,))] * 2,
    )
    fetched = exchange(served.reshape(count, cap, width), ALL).reshape(slots, width)

    reordered, natural, weight = call(
        functools.partial(ready, cols=cols),
        (pltpu.HBM((hidden, hidden), BF), pltpu.HBM((hidden, hidden), BF), pltpu.HBM((2 * width, hidden), BF)),
        (4 * width * hidden * hidden, 12 * hidden * hidden),
        core[None], w_self1, w_nbr1, limit=24,
    )
    one, many, share = call(
        functools.partial(mark, tile=16, cap=cap),
        (pltpu.HBM((nodes, slots), BF), pltpu.HBM((nodes, slots), BF), pltpu.HBM((nodes, 128), F32)),
        (nodes * slots * 48, 4 * nodes * slots),
        nbr_ids.T, self_ids[None], hop_counts[None], miss_counts.reshape(1, count), limit=24,
        scratch=[pltpu.VMEM((16, slots), BF), pltpu.VMEM((nodes, 128), jnp.int32)],
    )
    back, turned = call(
        spread_back,
        (pltpu.HBM((nodes, hidden), F32), pltpu.HBM((hosts * seeds, hidden), BF)),
        (8 * seeds * hidden * hidden, 12 * hidden * hidden),
        reordered, w_self2, w_nbr2, seed_counts[:, None], jnp.tile(seed_counts, 6)[None], *cots,
        limit=24,
    )

    held = (fetched, one, many, weight, back, natural, share)
    part = shape((seeds, 2 * hidden // hosts), BF)
    rows_one, grad, both, *parts = call(
        functools.partial(layer, tile=nodes // 2),
        (
            pltpu.VMEM((nodes, 2 * width), BF), pltpu.VMEM((nodes, hidden), BF),
            shape((seeds, 2 * hidden), BF), part, part, part, part,
        ),
        (4 * nodes * slots * width, 8 * nodes * slots),
        h[None], *held, seed_counts[:, None],
        far=tuple(range(1, 1 + len(held))), limit=40,
        scratch=[pltpu.VMEM(x.shape, x.dtype) for x in held]
        + [pltpu.VMEM((nodes, hidden), BF), pltpu.SemaphoreType.DMA((len(held),))],
    )

    parts = parts[:1] + [along_z(parts[k], k, hosts) for k in range(1, hosts)]
    give = call(
        give_one, shape((hidden // 2, 2 * width), BF),
        (2 * nodes * hidden * width, 4 * hidden * width), grad, rows_one,
        near=(0, 1), limit=16,
    )
    taken = swap_pair(give, devs)
    give = call(
        give_two, shape((hidden // 2, 2 * hidden // hosts), BF),
        (4 * hidden * hidden * seeds, hidden * hidden), turned, *parts,
    )
    taken_two = swap_pair(give, devs)
    tall = 2 * width + 2 * hidden // hosts
    part = call(
        functools.partial(stay, steps=2), Left((hidden // 2, tall), BF),
        (2 * nodes * hidden * width, 4 * hidden * width), grad, rows_one, taken, turned, taken_two,
        *parts, near=(0, 1), limit=24,
        scratch=[pltpu.VMEM((hidden // 2, tall), BF), pltpu.SemaphoreType.DMA((2,))],
    )
    part = exchange(part.reshape(count // 2, cols, tall), ALL, parity_groups(hosts, devs))

    embedding = (product(both[:, :hidden], w_self2) + product(both[:, hidden:], w_nbr2)).astype(BF)
    narrow, broad = shape((cols, width), F32), shape((cols, hidden), F32)
    sums = call(
        functools.partial(total, hosts=hosts), (narrow, narrow, broad, broad),
        (count * cols * tall, count * cols * tall), part, far=(0,), limit=16,
        scratch=[pltpu.VMEM(part.shape, BF), pltpu.SemaphoreType.DMA((hosts,))],
    )
    return (embedding, moved[None]) + tuple(x.T for x in sums)


def solution(mesh):
    return jax.shard_map(
        step,
        mesh=mesh,
        in_specs=(
            P(ALL, None), P("hst", "dev", None), P("hst", "dev"), P(ALL, None, None, None),
            P(ALL, None, None), P(ALL), P(ALL, None), P(ALL), P(ALL), P(), P(), P(), P(),
            P(ALL, None),
        ),
        out_specs=(
            P(ALL, None), P("hst", "dev", None), P(None, ALL), P(None, ALL), P(None, ALL),
            P(None, ALL),
        ),
        check_vma=False,
    )
```

```python
import functools

import jax
import jax.numpy as jnp
from jax import lax
from jax.experimental import pallas as pl
from jax.experimental.pallas import tpu as pltpu
from jax.sharding import PartitionSpec as P


FAN1 = 25
FAN2 = 15
CSLOT = 2
BLOCK = 128
ALL = ("hst", "dev")
BF = jnp.bfloat16
F32 = jnp.float32


def parity_groups(hosts, devs):
    return [
        [h * devs + 2 * i + c for h in range(hosts) for i in range(devs // 2)] for c in range(2)
    ]


def exchange(x, axes, groups=None):
    return lax.all_to_all(
        x, axes, split_axis=0, concat_axis=0, tiled=True, axis_index_groups=groups
    )


def swap_pair(x, devs):
    return lax.ppermute(x, "dev", [(i, i ^ 1) for i in range(devs)])


def along_z(x, k, hosts):
    return lax.ppermute(x, "hst", [(i, (i + k) % hosts) for i in range(hosts)])


class Left:
    def __init__(self, shape, kind):
        self.ref = pltpu.HBM(shape, kind)


def is_left(x):
    return isinstance(x, Left)


def call(body, outs, cost, *args, near=(), far=(), scratch=(), limit=8):
    space = pl.BlockSpec(memory_space=pltpu.VMEM)
    scalar = pl.BlockSpec(memory_space=pltpu.SMEM)
    away = pl.BlockSpec(memory_space=pltpu.HBM)
    flops, traffic = cost
    kinds = [scalar if x.ndim == 1 else away if i in far else space for i, x in enumerate(args)]
    place = {**{i: pltpu.VMEM for i in near}, **{i: pltpu.HBM for i in far}}
    args = [
        pltpu.with_memory_space_constraint(x, place[i]) if i in place else x
        for i, x in enumerate(args)
    ]
    left = [isinstance(x, Left) for x in jax.tree.leaves(outs, is_leaf=is_left)]
    outs = jax.tree.map(lambda x: x.ref if is_left(x) else x, outs, is_leaf=is_left)
    tree = jax.tree.structure(outs)
    return pl.pallas_call(
        body,
        out_shape=outs,
        in_specs=kinds,
        out_specs=jax.tree.unflatten(tree, [away if x else space for x in left]),
        scratch_shapes=scratch,
        cost_estimate=pl.CostEstimate(flops=flops, transcendentals=0, bytes_accessed=traffic),
        compiler_params=pltpu.CompilerParams(vmem_limit_bytes=limit << 20),
    )(*args)


def product(a, b):
    return jnp.dot(a, b, preferred_element_type=F32)


def across(a, b):
    return lax.dot_general(a, b, (((0,), (0,)), ((), ())), preferred_element_type=F32)


def along(a, b):
    return lax.dot_general(a, b, (((1,), (1,)), ((), ())), preferred_element_type=F32)


def pack(plan_ref, ids_hbm, block_hbm, out_ref, ids_ref, block_ref, sems, *, sub):
    devs, _, _ = out_ref.shape
    groups = devs // 2
    half = block_ref.shape[1] // 2
    load_ids = pltpu.make_async_copy(ids_hbm, ids_ref, sems.at[0])
    load_block = pltpu.make_async_copy(block_hbm, block_ref, sems.at[1])
    load_ids.start()
    load_block.start()
    load_ids.wait()
    hosts, cap, _ = ids_ref.shape
    line = lax.broadcasted_iota(jnp.int32, (cap, 128), 0)
    lane = lax.broadcasted_iota(jnp.int32, (cap, 128), 1)
    to_high = (lane == line).astype(F32).astype(BF)
    to_low = (lane == line + cap).astype(F32).astype(BF)
    row = lax.broadcasted_iota(jnp.int32, (devs, sub, 128), 1)
    lane = lax.broadcasted_iota(jnp.int32, (devs, sub, 128), 2)
    note = jnp.zeros((devs, sub, 128), F32)
    for k in range(hosts):
        ids = ids_ref[k]
        high = (ids // 256).astype(F32).astype(BF)
        low = (ids % 256).astype(F32).astype(BF)
        part = across(high, to_high) + across(low, to_low)
        note = jnp.where(row == k, part[:, None, :], note)
    for j in range(CSLOT):
        note = jnp.where(lane == 64 + j, plan_ref[j].astype(F32), note)
    out_ref[:, :, CSLOT * half :] = note.astype(BF)
    load_block.wait()
    block = block_ref[...].astype(F32).reshape(CSLOT, groups, sub, 2 * half)
    for j in range(2):
        for i in range(CSLOT):
            piece = block[i, :, :, j * half : (j + 1) * half].astype(BF)
            out_ref[j * groups : (j + 1) * groups, :, i * half : (i + 1) * half] = piece


def serve(asked_ref, got_ref, stored_hbm, out_hbm, stored_ref, out_ref, in_sems, out_sems, *,
          rows_dev, sub, tile):
    steps = stored_ref.shape[0] // tile
    span = got_ref.shape[0] // 2
    half = got_ref.shape[1]
    block = span // CSLOT
    ones = jnp.ones((span, 128), BF)
    chunks = [pl.ds(t * tile, tile) for t in range(steps)]
    loads = [
        pltpu.make_async_copy(stored_hbm.at[c, :], stored_ref.at[c, :], in_sems.at[t])
        for t, c in enumerate(chunks)
    ]
    stores = [
        pltpu.make_async_copy(out_ref.at[c, :], out_hbm.at[c, :], out_sems.at[t])
        for t, c in enumerate(chunks)
    ]
    for load in loads:
        load.start()
    for t in range(steps):
        rows = slice(t * tile, (t + 1) * tile)
        row = asked_ref[:, rows] - rows_dev
        inner = row % block
        place = (inner // sub) * (CSLOT * sub) + (row // block) * sub + inner % sub
        place = jnp.where(row >= 0, place, -1)
        pick = (place == lax.broadcasted_iota(jnp.int32, (span, tile), 0)).astype(F32)
        pick = pick.astype(BF)
        hit = across(pick, ones) > 0.5
        cached = [across(pick, got_ref[j * span : (j + 1) * span, :]) for j in range(2)]
        loads[t].wait()
        for j in range(2):
            for i in range(half // 128):
                cols = slice(j * half + i * 128, j * half + (i + 1) * 128)
                stored = stored_ref[rows, cols].astype(F32)
                cell = jnp.where(hit, cached[j][:, i * 128 : (i + 1) * 128], stored)
                out_ref[rows, cols] = cell.astype(BF)
        stores[t].start()
    for store in stores:
        store.wait()


def sort(host_ref, got_ref, pieces_ref, *part_refs, sub):
    devs, _, tall = got_ref.shape
    hosts = len(part_refs)
    half = (tall - 128) // CSLOT
    rows = devs * CSLOT * sub
    note = got_ref[:, :, CSLOT * half :].astype(F32)
    block = jnp.concatenate(
        [
            jnp.broadcast_to(note[:, :, 64 + j : 65 + j], (devs, sub, 128)).reshape(devs, 1, sub, 128)
            for j in range(CSLOT)
        ],
        1,
    ).reshape(rows, 128)
    block = block.astype(jnp.int32)
    inner = lax.broadcasted_iota(jnp.int32, (rows, 128), 0) % sub
    lane = lax.broadcasted_iota(jnp.int32, (rows, 128), 1)
    total = jnp.zeros((rows, half), F32)
    for j in range(CSLOT):
        source = jnp.where(block % CSLOT == j, block // CSLOT * sub + inner, -1)
        pick = jnp.concatenate(
            [(source == lane + i * 128).astype(F32) for i in range(devs * sub // 128)], 1
        ).astype(BF)
        piece = got_ref[:, :, j * half : (j + 1) * half].astype(F32).reshape(devs * sub, half)
        total = total + product(pick, piece.astype(BF))
    pieces_ref[...] = total.astype(BF)
    line = lax.broadcasted_iota(jnp.int32, note.shape, 1)
    for k in range(hosts):
        host = (host_ref[0] + k) % hosts
        part_refs[k][...] = jnp.sum(jnp.where(line == host, note, 0.0), 1).astype(BF)


def decode(host_ref, *refs, cap, top):
    parts, (asked_ref, stored_ref) = refs[:-2], refs[-2:]
    hosts = len(parts)
    devs = parts[0].shape[0]
    span = devs * cap
    lane = lax.broadcasted_iota(jnp.int32, (devs, span), 1)
    spread = (lane // cap == lax.broadcasted_iota(jnp.int32, (devs, span), 0)).astype(F32)
    spread = spread.astype(BF)
    line = lax.broadcasted_iota(jnp.int32, (128, span), 0)
    place = lax.broadcasted_iota(jnp.int32, (128, span), 1) % cap
    scale = jnp.where(line == place, 256.0, jnp.where(line == place + cap, 1.0, 0.0))
    found = []
    for part in parts:
        ids = across(part[...], spread) * scale
        found.append(jnp.sum(ids, 0, keepdims=True).astype(jnp.int32))
    for j in range(hosts):
        turn = (host_ref[0] - j + hosts) % hosts
        row = found[0]
        for k in range(1, hosts):
            row = jnp.where(turn == k, found[k], row)
        asked_ref[:, j * span : (j + 1) * span] = row
        stored_ref[:, j * span : (j + 1) * span] = jnp.minimum(row, top)


def mark(near_ref, self_ref, hop_ref, count_ref, one_ref, many_ref, share_ref, used_ref,
         table_ref, *, tile, cap):
    nodes, slots = one_ref.shape
    peers = count_ref.shape[1]
    lane = lax.broadcasted_iota(jnp.int32, (peers, slots), 1)
    spread = lane // cap == lax.broadcasted_iota(jnp.int32, (peers, slots), 0)
    counts = jnp.broadcast_to(count_ref[...].astype(F32), (16, peers)).astype(BF)
    counts = product(counts, spread.astype(F32).astype(BF))
    rank = lax.broadcasted_iota(jnp.int32, counts.shape, 1) % cap
    used_ref[...] = (rank.astype(F32) < counts).astype(F32).astype(BF)

    hop = hop_ref[...]
    near = near_ref[...]
    near = jnp.where(lax.broadcasted_iota(jnp.int32, near.shape, 0) < hop, near, slots)
    rows = jnp.concatenate([near, self_ref[...]], 0)
    high = (rows // 256).astype(F32).astype(BF)
    low = (rows % 256).astype(F32).astype(BF)
    lines = rows.shape[0]
    turn = lax.broadcasted_iota(jnp.int32, (lines, 128), 0)
    turn = (turn == lax.broadcasted_iota(jnp.int32, (lines, 128), 1)).astype(F32).astype(BF)
    table_ref[...] = (256.0 * across(high, turn) + across(low, turn)).astype(jnp.int32)
    all_hop = jnp.broadcast_to(hop.astype(F32), (16, nodes)).astype(BF)
    first = lax.broadcasted_iota(jnp.int32, (16, 128), 0) == 0
    share_ref[...] = 1.0 / across(all_hop, first.astype(F32).astype(BF))
    kind = jnp.int16

    def step(i, carry):
        rows = pl.ds(i * tile, tile)
        table = table_ref[rows, :]
        named = [
            jnp.broadcast_to(table[:, k : k + 1], (tile, 128)).astype(kind)
            for k in range(FAN2 + 1)
        ]
        lane = lax.broadcasted_iota(jnp.int32, (tile, 128), 1)
        yes, no = jnp.ones((tile, 128), BF), jnp.zeros((tile, 128), BF)
        for j in range(slots // 128):
            cols = slice(j * 128, (j + 1) * 128)
            slot = (lane + j * 128).astype(kind)
            live = used_ref[:, cols]
            one_ref[rows, cols] = jnp.where(named[FAN2] == slot, yes, no) * live
            total = jnp.where(named[0] == slot, yes, no)
            for k in range(1, FAN2):
                total = total + jnp.where(named[k] == slot, yes, no)
            many_ref[rows, cols] = total * live
        return carry

    lax.fori_loop(0, nodes // tile, step, 0)


def ready(core_ref, self1_ref, nbr1_ref, order_ref, natural_ref, weight_ref, *, cols):
    width = self1_ref.shape[0]
    hidden = order_ref.shape[0]
    pos = lax.broadcasted_iota(jnp.int32, (1, hidden), 1)
    inner = pos % (hidden // 2)
    side = jnp.where(pos < hidden // 2, 1 - core_ref[0], core_ref[0])
    source = (inner // cols) * (2 * cols) + side * cols + inner % cols
    hot = source == lax.broadcasted_iota(jnp.int32, (hidden, hidden), 0)
    order_ref[...] = hot.astype(F32).astype(BF)
    block = pos // cols
    place = jnp.where(block % 2 == core_ref[0], hidden // 2, 0) + block // 2 * cols + pos % cols
    hot = place == lax.broadcasted_iota(jnp.int32, (hidden, hidden), 0)
    natural_ref[...] = hot.astype(F32).astype(BF)
    weight_ref[:width, :] = product(self1_ref[...], order_ref[...]).astype(BF)
    weight_ref[width:, :] = product(nbr1_ref[...], order_ref[...]).astype(BF)


def spread_back(order_ref, self2_ref, nbr2_ref, col_ref, row_ref, cot_ref, *refs):
    others, (back_ref, turned_ref) = refs[:-2], refs[-2:]
    rows = jnp.concatenate([cot_ref[...]] + [r[...] for r in others], 0)
    turned_ref[...] = product(rows, order_ref[...]).astype(BF)
    seeds = cot_ref.shape[0]
    nodes = back_ref.shape[0]
    back_self = along(cot_ref[...], self2_ref[...])
    back_mean = along(cot_ref[...], nbr2_ref[...]) / col_ref[...].astype(F32)
    rest = jnp.concatenate([back_self, back_mean], 0)
    pieces = []
    for _ in range(3):
        piece = rest.astype(BF)
        rest = rest - piece.astype(F32)
        pieces.append(piece)
    lane = lax.broadcasted_iota(jnp.int32, (1, 6 * seeds), 1) % (2 * seeds)
    seed = lane % seeds
    first = jnp.where(lane < seeds, seed, seeds + seed * FAN1)
    last = jnp.where(lane < seeds, seed + 1, first + row_ref[...])
    node = lax.broadcasted_iota(jnp.int32, (nodes, 6 * seeds), 0)
    spread = ((node >= first) & (node < last)).astype(F32).astype(BF)
    pieces = product(jnp.concatenate(pieces, 0), order_ref[...]).astype(BF)
    back_ref[...] = product(spread, pieces)


def layer(host_ref, fetched_hbm, one_hbm, many_hbm, weight_hbm, back_hbm, natural_hbm, share_hbm, col_ref,
          rows_ref, grad_ref, pair_ref, part0_ref, part1_ref, part2_ref, part3_ref,
          fetched_ref, one_ref, many_ref, weight_ref, back_ref, natural_ref, share_ref, hid_ref, sems, *, tile):
    away = (fetched_hbm, one_hbm, many_hbm, weight_hbm, back_hbm, natural_hbm, share_hbm)
    held = (fetched_ref, one_ref, many_ref, weight_ref, back_ref, natural_ref, share_ref)
    loads = [pltpu.make_async_copy(a, b, sems.at[i]) for i, (a, b) in enumerate(zip(away, held))]
    for i in (0, 1, 2, 6, 3, 4, 5):
        loads[i].start()
    nodes = one_ref.shape[0]
    width = fetched_ref.shape[1]
    seeds = col_ref.shape[0]
    hidden = weight_ref.shape[1]
    loads[0].wait()
    loads[1].wait()
    for i in range(nodes // tile):
        rows = slice(i * tile, (i + 1) * tile)
        rows_ref[rows, :width] = product(one_ref[rows, :], fetched_ref[...]).astype(BF)
        if i == 0:
            loads[2].wait()
            loads[6].wait()
        total = product(many_ref[rows, :], fetched_ref[...])
        rows_ref[rows, width:] = (total * share_ref[rows, :1]).astype(BF)
        if i == 0:
            loads[3].wait()
            loads[4].wait()
        pre = product(rows_ref[rows, :], weight_ref[...])
        gate = 1.0 / (1.0 + jnp.exp(-pre))
        hid_ref[rows, :] = (pre * gate).astype(BF)
        grad_ref[rows, :] = (back_ref[rows, :] * gate * (1.0 + pre * (1.0 - gate))).astype(BF)
    loads[5].wait()
    node = lax.broadcasted_iota(jnp.int32, (seeds, nodes), 1)
    first = seeds + lax.broadcasted_iota(jnp.int32, (seeds, nodes), 0) * FAN1
    live = ((node >= first) & (node < first + col_ref[...])).astype(F32).astype(BF)
    mean = (product(live, hid_ref[...]) / col_ref[...].astype(F32)).astype(BF)
    both = product(jnp.concatenate([hid_ref[:seeds, :], mean], 0), natural_ref[...]).astype(BF)
    pair_ref[:, :hidden] = both[:seeds, :]
    pair_ref[:, hidden:] = both[seeds:, :]
    parts = (part0_ref, part1_ref, part2_ref, part3_ref)
    slab = hidden // len(parts)
    for k in range(len(parts)):
        start = pl.multiple_of((host_ref[0] + k) % len(parts) * slab, slab)
        parts[k][:, :slab] = pair_ref[:, pl.ds(start, slab)]
        parts[k][:, slab:] = pair_ref[:, pl.ds(hidden + start, slab)]


def give_one(grad_ref, rows_ref, give_ref):
    hidden = grad_ref.shape[1]
    give_ref[...] = across(grad_ref[:, : hidden // 2], rows_ref[...]).astype(BF)


def give_two(cot_ref, *refs):
    parts, give_ref = refs[:-1], refs[-1]
    rows = jnp.concatenate([p[...] for p in parts], 0)
    give_ref[...] = across(cot_ref[:, : cot_ref.shape[1] // 2], rows).astype(BF)


def hold(grad_ref, rows_ref, cot_ref, *refs):
    parts, kept_ref = refs[:-1], refs[-1]
    half = grad_ref.shape[1] // 2
    wide = rows_ref.shape[1]
    kept_ref[:, :wide] = across(grad_ref[:, half:], rows_ref[...])
    rows = jnp.concatenate([p[...] for p in parts], 0)
    kept_ref[:, wide:] = across(cot_ref[:, half:], rows)


def stay(kept_ref, taken_ref, taken2_ref, out_hbm, out_ref, sems, *, steps):
    wide = taken_ref.shape[1]
    tile = kept_ref.shape[0] // steps
    stores = []
    for t in range(steps):
        chunk = slice(t * tile, (t + 1) * tile)
        out_ref[chunk, :wide] = (kept_ref[chunk, :wide] + taken_ref[chunk, :].astype(F32)).astype(BF)
        out_ref[chunk, wide:] = (kept_ref[chunk, wide:] + taken2_ref[chunk, :].astype(F32)).astype(BF)
        window = pl.ds(t * tile, tile)
        stores.append(
            pltpu.make_async_copy(out_ref.at[window, :], out_hbm.at[window, :], sems.at[t])
        )
        stores[-1].start()
    for store in stores:
        store.wait()


def total(part_hbm, self1_ref, nbr1_ref, self2_ref, nbr2_ref, part_ref, sems, *, hosts):
    sources = part_hbm.shape[0] // hosts
    width = self1_ref.shape[1]
    slab = self2_ref.shape[1] // hosts
    loads = []
    for i in range(hosts):
        window = pl.ds(i * sources, sources)
        loads.append(pltpu.make_async_copy(part_hbm.at[window], part_ref.at[window], sems.at[i]))
        loads[-1].start()
    for i in range(hosts):
        loads[i].wait()
        group = slice(i * sources, (i + 1) * sources)

        def add(start, size):
            return jnp.sum(part_ref[group, :, start : start + size].astype(F32), 0)

        if i == 0:
            self1_ref[...] = add(0, width)
            nbr1_ref[...] = add(width, width)
        else:
            self1_ref[...] += add(0, width)
            nbr1_ref[...] += add(width, width)
        cols = slice(i * slab, (i + 1) * slab)
        self2_ref[:, cols] = add(2 * width, slab)
        nbr2_ref[:, cols] = add(2 * width + slab, slab)


def step(
    features, cache_blocks, plan, miss_ids, miss_counts, self_ids, nbr_ids, hop_counts,
    seed_counts, w_self1, w_nbr1, w_self2, w_nbr2, cotangent,
):
    hosts = lax.axis_size("hst")
    devs = lax.axis_size("dev")
    count = hosts * devs
    rows_dev, width = features.shape
    hidden = w_self2.shape[0]
    cap = miss_ids.shape[3]
    nodes = self_ids.shape[0]
    seeds = seed_counts.shape[0]
    h = lax.axis_index("hst")
    d = lax.axis_index("dev")
    core = d % 2
    half = width // 2
    groups = devs // 2
    sub = BLOCK // groups
    slots = count * cap
    cols = hidden // count
    shape = jax.ShapeDtypeStruct

    tall = CSLOT * half + 128
    ids, block = miss_ids[0].transpose(0, 2, 1), cache_blocks[0]
    got = call(
        functools.partial(pack, sub=sub), pltpu.HBM((devs, sub, tall), BF),
        (16 * devs * sub * tall, 4 * devs * sub * tall), plan.reshape(CSLOT), ids, block,
        far=(1, 2),
        scratch=[pltpu.VMEM(x.shape, x.dtype) for x in (ids, block)]
        + [pltpu.SemaphoreType.DMA((2,))],
    )
    got = exchange(got, "dev")

    cots = [cotangent] + [along_z(cotangent, k, hosts) for k in range(1, hosts)]
    got, cots = lax.optimization_barrier((got, cots))

    line = shape((devs, 128), BF)
    pieces, *parts = call(
        functools.partial(sort, sub=sub),
        (pltpu.HBM((devs * CSLOT * sub, half), BF),) + (line,) * hosts,
        (2 * devs * devs * CSLOT * CSLOT * sub * sub * half, 8 * devs * half),
        h[None], got,
    )
    parts = parts[:1] + [along_z(parts[k], k, hosts) for k in range(1, hosts)]
    pieces = exchange(pieces.reshape(devs, CSLOT * sub, half), "dev")
    moved = (
        pieces.reshape(2, groups, CSLOT, sub, half)
        .transpose(2, 1, 3, 0, 4)
        .reshape(CSLOT * BLOCK, width)
    )

    line = shape((1, slots), jnp.int32)
    asked, kept = call(
        functools.partial(decode, cap=cap, top=rows_dev - 1), (line, line),
        (slots * devs * 256, 64 * slots), h[None], *parts,
    )
    stored = features.at[kept.reshape(slots)].get(mode="promise_in_bounds")
    tile = 256
    served = call(
        functools.partial(serve, rows_dev=rows_dev, sub=sub, tile=tile),
        Left((slots, width), BF), (4 * slots * CSLOT * BLOCK * width, 4 * slots * width),
        asked, pieces.reshape(2 * CSLOT * BLOCK, half), stored, far=(2,), limit=16,
        scratch=[pltpu.VMEM((slots, width), BF)] * 2
        + [pltpu.SemaphoreType.DMA((slots // tile,))] * 2,
    )
    fetched = exchange(served.reshape(count, cap, width), ALL).reshape(slots, width)

    reordered, natural, weight = call(
        functools.partial(ready, cols=cols),
        (pltpu.HBM((hidden, hidden), BF), pltpu.HBM((hidden, hidden), BF), pltpu.HBM((2 * width, hidden), BF)),
        (4 * width * hidden * hidden, 12 * hidden * hidden),
        core[None], w_self1, w_nbr1, limit=24,
    )
    one, many, share = call(
        functools.partial(mark, tile=16, cap=cap),
        (pltpu.HBM((nodes, slots), BF), pltpu.HBM((nodes, slots), BF), pltpu.HBM((nodes, 128), F32)),
        (nodes * slots * 48, 4 * nodes * slots),
        nbr_ids.T, self_ids[None], hop_counts[None], miss_counts.reshape(1, count), limit=24,
        scratch=[pltpu.VMEM((16, slots), BF), pltpu.VMEM((nodes, 128), jnp.int32)],
    )
    back, turned = call(
        spread_back,
        (pltpu.HBM((nodes, hidden), F32), pltpu.HBM((hosts * seeds, hidden), BF)),
        (8 * seeds * hidden * hidden, 12 * hidden * hidden),
        reordered, w_self2, w_nbr2, seed_counts[:, None], jnp.tile(seed_counts, 6)[None], *cots,
        limit=24,
    )

    held = (fetched, one, many, weight, back, natural, share)
    part = shape((seeds, 2 * hidden // hosts), BF)
    rows_one, grad, both, *parts = call(
        functools.partial(layer, tile=nodes // 2),
        (
            pltpu.VMEM((nodes, 2 * width), BF), pltpu.VMEM((nodes, hidden), BF),
            shape((seeds, 2 * hidden), BF), part, part, part, part,
        ),
        (4 * nodes * slots * width, 8 * nodes * slots),
        h[None], *held, seed_counts[:, None],
        far=tuple(range(1, 1 + len(held))), limit=40,
        scratch=[pltpu.VMEM(x.shape, x.dtype) for x in held]
        + [pltpu.VMEM((nodes, hidden), BF), pltpu.SemaphoreType.DMA((len(held),))],
    )

    parts = parts[:1] + [along_z(parts[k], k, hosts) for k in range(1, hosts)]
    give = call(
        give_one, shape((hidden // 2, 2 * width), BF),
        (2 * nodes * hidden * width, 4 * hidden * width), grad, rows_one,
        near=(0, 1), limit=16,
    )
    taken = swap_pair(give, devs)
    give = call(
        give_two, shape((hidden // 2, 2 * hidden // hosts), BF),
        (4 * hidden * hidden * seeds, hidden * hidden), turned, *parts,
    )
    taken_two = swap_pair(give, devs)
    tall = 2 * width + 2 * hidden // hosts
    parts, _ = lax.optimization_barrier((parts, give))
    kept = call(
        hold, pltpu.VMEM((hidden // 2, tall), F32),
        (2 * nodes * hidden * width, 4 * hidden * width), grad, rows_one, turned, *parts,
        near=(0, 1), limit=24,
    )
    part = call(
        functools.partial(stay, steps=4), Left((hidden // 2, tall), BF),
        (hidden * tall, 4 * hidden * tall), kept, taken, taken_two, near=(0,), limit=24,
        scratch=[pltpu.VMEM((hidden // 2, tall), BF), pltpu.SemaphoreType.DMA((4,))],
    )
    part = exchange(part.reshape(count // 2, cols, tall), ALL, parity_groups(hosts, devs))

    embedding = (product(both[:, :hidden], w_self2) + product(both[:, hidden:], w_nbr2)).astype(BF)
    narrow, broad = shape((cols, width), F32), shape((cols, hidden), F32)
    sums = call(
        functools.partial(total, hosts=hosts), (narrow, narrow, broad, broad),
        (count * cols * tall, count * cols * tall), part, far=(0,), limit=16,
        scratch=[pltpu.VMEM(part.shape, BF), pltpu.SemaphoreType.DMA((hosts,))],
    )
    return (embedding, moved[None]) + tuple(x.T for x in sums)


def solution(mesh):
    return jax.shard_map(
        step,
        mesh=mesh,
        in_specs=(
            P(ALL, None), P("hst", "dev", None), P("hst", "dev"), P(ALL, None, None, None),
            P(ALL, None, None), P(ALL), P(ALL, None), P(ALL), P(ALL), P(), P(), P(), P(),
            P(ALL, None),
        ),
        out_specs=(
            P(ALL, None), P("hst", "dev", None), P(None, ALL), P(None, ALL), P(None, ALL),
            P(None, ALL),
        ),
        check_vma=False,
    )
```
